32 devices in a mesh: pocket: 16 (over z, y, x), tensor: 2 (over core).
Axes of the slice: x: 2, y: 2, z: 4, core: 2. Of those that a mesh axis runs over, the one named last changes fastest.
Arguments:
- z_home: bfloat16 [48, 32, 256], P('pocket'), may hold values from -6 to 6
- counts: int32 [48], replicated, may hold values from 1 to 32, as said below
- table: int32 [48, 32], replicated, may hold values from 0 to 575, as said below
- keys: bfloat16 [48, 1536, 128], P('pocket', 'tensor'), may hold values from -2500 to 2500, as said below
- values: bfloat16 [48, 1536, 128], P('pocket', 'tensor'), may hold values from -6 to 6
- w_embed: float32 [16, 1536], replicated, may hold values from -1.5 to 1.5
- step_bias: float32 [4, 1536], replicated, may hold values from -6 to 6
- ln_gain: float32 [1536], replicated, may hold values from 0.1 to 1.9
- w_query: bfloat16 [1536, 1536], P('tensor'), may hold values from -0.15625 to 0.15625
- w_out: bfloat16 [1536, 16], P('tensor'), may hold values from -0.15625 to 0.15625
Outputs:
- denoised: float32 [576, 256], P('pocket')
The draws below stay inside these ranges and needn't reach their ends.
Inputs may be any that keep to these rules, and one draw needn't show every extreme that they name: `counts`: each pocket holds 1 to 32 samples. On half of the devices of the pocket axis the 3 pockets of a device hold 44 samples together, one of them exactly 32; on the other half they hold 28. `table`: positions s < counts[p] of pocket p are live and name distinct work slots that cover all 576; slot g lies on device g // 36 of the pocket axis. Entries at other positions are arbitrary and unused. A device keeps its own live samples up to 36; a device with 44 hands exactly one sample to each device that holds 28, and no device hands more than 1 to another. `keys`: finite values.
All inputs are finite; a program needn't handle non-finite values.
Results may differ from the reference program's by a relative error of at most 0.017.
The reference program's roundings to bfloat16 on the way (of `normed`, `queries`, `weight` and `attended`) count: a program that leaves them out, or rounds other values in their place, can miss the bound.
Values may be sent and summed in bfloat16 or wider, within the bound.
A program may use at most 64 MiB of HBM per device.

```python
import math
import jax
import jax.numpy as jnp
from jax import lax

D = 1536
HEADS = 24
HEAD = 64
CH = 16
LIG = 16
PRES = 128
STEPS = 4
P_DEV = 3
SMAX = 32
CAP = 1
WORK = 36
MOVE = 8
POCKETS = 48
SLOTS = 576


def sample_plan(key):
    base_key = jax.random.fold_in(key, 4321)
    role_key, split_key, spot_key, keep_key, slot_key, junk_key = jax.random.split(base_key, 6)
    device_count = POCKETS // P_DEV
    half_count = device_count // 2
    role_rank = jax.random.permutation(role_key, device_count).astype(jnp.int32)
    heavy = role_rank < half_count
    role_order = jnp.argsort(role_rank).astype(jnp.int32)
    load_size = jnp.where(heavy, WORK + MOVE, WORK - MOVE)
    remaining = load_size - jnp.where(heavy, SMAX, 0)
    free_number = jnp.where(heavy, P_DEV - 1, P_DEV)
    split_keys = jax.random.split(split_key, P_DEV)
    pieces = []
    for pocket_slot in range(P_DEV):
        after_count = free_number - pocket_slot - 1
        active = pocket_slot < free_number
        lower = jnp.maximum(1, remaining - after_count * SMAX)
        upper = jnp.minimum(SMAX, remaining - after_count)
        picked = jax.random.randint(split_keys[pocket_slot], (device_count,), lower, jnp.maximum(upper, lower) + 1)
        picked = jnp.where(active, picked, 0)
        pieces.append(picked)
        remaining = remaining - picked
    free_counts = jnp.stack(pieces, axis=1)
    forced_line = jnp.concatenate([jnp.full((device_count, 1), SMAX, jnp.int32), free_counts[:, :P_DEV - 1]], axis=1)
    lined = jnp.where(heavy[:, None], forced_line, free_counts)
    spot_index = jax.random.randint(spot_key, (device_count,), 0, P_DEV)
    gather_index = (jnp.arange(P_DEV, dtype=jnp.int32)[None, :] - spot_index[:, None]) % P_DEV
    count_table = jnp.take_along_axis(lined, gather_index, axis=1).astype(jnp.int32)
    entry_count = P_DEV * SMAX
    live_mask = (jnp.arange(SMAX, dtype=jnp.int32)[None, None, :] < count_table[:, :, None]).reshape(device_count, entry_count)
    live_rank = jnp.cumsum(live_mask.astype(jnp.int32), axis=1) - 1

    def permute_keep(draw_key):
        return jax.random.permutation(draw_key, WORK + MOVE)

    def permute_slot(draw_key):
        return jax.random.permutation(draw_key, WORK)
    keep_order = jax.vmap(permute_keep)(jax.random.split(keep_key, device_count)).astype(jnp.int32)
    slot_order = jax.vmap(permute_slot)(jax.random.split(slot_key, device_count)).astype(jnp.int32)
    clipped_rank = jnp.clip(live_rank, 0, WORK + MOVE - 1)
    shuffled = jnp.take_along_axis(keep_order, clipped_rank, axis=1)
    device_ids = jnp.arange(device_count, dtype=jnp.int32)[:, None]
    kept_heavy = device_ids * WORK + jnp.take_along_axis(slot_order, jnp.clip(shuffled, 0, WORK - 1), axis=1)
    moved_index = jnp.clip(shuffled - WORK, 0, MOVE - 1)
    light_device = role_order[half_count + moved_index // CAP]
    arrival_index = role_rank[:, None] * CAP + moved_index % CAP
    arrival_slot = slot_order[light_device, WORK - MOVE + arrival_index]
    moved_heavy = light_device * WORK + arrival_slot
    heavy_value = jnp.where(shuffled < WORK, kept_heavy, moved_heavy)
    light_value = device_ids * WORK + jnp.take_along_axis(slot_order, jnp.clip(live_rank, 0, WORK - 1), axis=1)
    slot_value = jnp.where(heavy[:, None], heavy_value, light_value)
    junk_value = jax.random.randint(junk_key, (device_count, entry_count), 0, device_count * WORK)
    slot_table = jnp.where(live_mask, slot_value, junk_value).astype(jnp.int32)
    return (count_table.reshape(POCKETS), slot_table.reshape(POCKETS, SMAX))


def draw_counts(key, part):
    return sample_plan(key)[0]


def draw_table(key, part):
    return sample_plan(key)[1]


def draw_keys(key, part):
    base = jnp.clip(jax.random.normal(key, (POCKETS, PRES, D), jnp.float32), -6.0, 6.0)
    return jnp.swapaxes(base, 1, 2).astype(jnp.bfloat16)


def levels(rng, dims, shards, smallest, top_value):
    def one(position, parts):
        draws = jax.random.uniform(jax.random.fold_in(jax.random.fold_in(rng, 6), position), (parts,), jnp.float32, smallest / len(shards), top_value / len(shards))
        return jnp.repeat(jnp.exp(draws), dims[position] // parts).reshape((-1,) + (1,) * (len(dims) - position - 1))

    gain = one(*shards[0])
    for cut in shards[1:]:
        gain = gain * one(*cut)
    return gain


def scatter_about(key, shape, scale, most, shards=(), held_as=jnp.bfloat16):
    array = jax.random.normal(key, shape, jnp.float32) * scale
    if len(shards) > 0:
        array = levels(key, shape, shards, -0.22, 0.18) * array
    return jnp.clip(array, min=-most, max=most).astype(held_as)


def setup_inputs(seed: int = 0) -> dict:
    seeds = jax.random.split(jax.random.key(seed), 11)
    z_home = scatter_about(seeds[0], (POCKETS, SMAX, LIG * CH), 1.0, 6.0, ((0, 16),))
    counts = draw_counts(jax.random.fold_in(seeds[10], 71), 0)
    table = draw_table(jax.random.fold_in(seeds[10], 71), 0)
    keys = draw_keys(jax.random.fold_in(seeds[10], 71), 0)
    values = scatter_about(seeds[4], (POCKETS, D, PRES), 1.0, 6.0, ((0, 16), (1, 2)))
    w_embed = scatter_about(seeds[5], (CH, D), CH ** -0.5, 1.5, (), jnp.float32)
    step_bias = scatter_about(seeds[6], (STEPS, D), 1.0, 6.0, (), jnp.float32)
    ln_gain = jnp.clip(1.0 + 0.18 * jax.random.normal(seeds[7], (D,), jnp.float32), 0.1, 1.9)
    w_query = scatter_about(seeds[8], (D, D), D ** -0.5, 0.15625, ((0, 2),))
    w_out = scatter_about(seeds[9], (D, CH), D ** -0.5, 0.15625, ((0, 2),))
    return {"z_home": z_home, "counts": counts, "table": table, "keys": keys, "values": values, "w_embed": w_embed, "step_bias": step_bias, "ln_gain": ln_gain, "w_query": w_query, "w_out": w_out}


def layer_norm(hidden, ln_gain):
    mean_value = lax.optimization_barrier(jnp.mean(hidden, axis=-1, keepdims=True))
    centred = hidden - mean_value
    variance = lax.optimization_barrier(jnp.mean(centred * centred, axis=-1, keepdims=True))
    return centred * lax.rsqrt(variance + 1e-05) * ln_gain

def attend(queries, key_rows, value_rows):
    block_size, atom_count, width = queries.shape
    residue_count = key_rows.shape[2]
    q_four = queries.astype(jnp.float32).reshape(block_size, atom_count, HEADS, HEAD)
    k_four = key_rows.astype(jnp.float32).reshape(block_size, HEADS, HEAD, residue_count)
    v_four = value_rows.astype(jnp.float32).reshape(block_size, HEADS, HEAD, residue_count)
    scores = jnp.einsum('bihe,bher->bhir', q_four, k_four) * (1.0 / math.sqrt(HEAD))
    scores = scores - lax.optimization_barrier(jnp.max(scores, axis=-1, keepdims=True))
    weight = jnp.exp(scores)
    weight = (weight / lax.optimization_barrier(jnp.sum(weight, axis=-1, keepdims=True))).astype(jnp.bfloat16)
    mixture = jnp.einsum('bhir,bher->bihe', weight.astype(jnp.float32), v_four)
    return mixture.astype(jnp.bfloat16).reshape(block_size, atom_count, width)

def reference(z_home, counts, table, keys, values, w_embed, step_bias, ln_gain, w_query, w_out):
    slot_total = SLOTS
    entry_total = POCKETS * SMAX
    live_mask = (jnp.arange(SMAX, dtype=jnp.int32)[None, :] < counts[:, None]).reshape(-1)
    target_slot = jnp.where(live_mask, table.reshape(-1), slot_total).astype(jnp.int32)
    source_entry = jnp.zeros((slot_total + 1,), jnp.int32).at[target_slot].set(jnp.arange(entry_total, dtype=jnp.int32))[:slot_total]
    z_rows = z_home.reshape(entry_total, LIG * CH)
    w_query_t = w_query.T

    def run_block(block_source):
        pocket_index = (block_source // SMAX).astype(jnp.int32)
        key_rows = keys[pocket_index]
        value_rows = values[pocket_index]
        z_state = z_rows[block_source].astype(jnp.float32)
        for step_index in range(STEPS):
            hidden = jnp.dot(z_state.reshape(-1, CH), w_embed, precision=lax.Precision.HIGHEST) + step_bias[step_index]
            normed = layer_norm(hidden, ln_gain).astype(jnp.bfloat16)
            queries = jnp.dot(normed, w_query_t, preferred_element_type=jnp.float32).astype(jnp.bfloat16)
            attended = attend(queries.reshape(-1, LIG, D), key_rows, value_rows)
            noise_guess = jnp.dot(attended.reshape(-1, D), w_out, preferred_element_type=jnp.float32)
            z_state = (0.95 + 0.01 * step_index) * z_state + (-0.8 + 0.1 * step_index) * noise_guess.reshape(-1, LIG * CH)
        return z_state
    blocks = lax.map(run_block, source_entry.reshape(-1, WORK))
    return blocks.reshape(slot_total, LIG * CH)
```

```python
import functools

import jax
import jax.numpy as jnp
from jax import lax
from jax.experimental import pallas as pl
from jax.experimental.pallas import tpu as pltpu
from jax.sharding import PartitionSpec as P

HEAD = 64
CAP = 1
WORK = 36
GS = 8
EPS = 1e-05
F32 = jnp.float32
BF16 = jnp.bfloat16
HIGHEST = lax.Precision.HIGHEST
NT = (((1,), (1,)), ((), ()))
TN = (((0,), (0,)), ((), ()))


def iota(shape, axis):
    return lax.broadcasted_iota(jnp.int32, shape, axis)


def split3(value):
    high = value.astype(BF16).astype(F32)
    rest = value - high
    middle = rest.astype(BF16).astype(F32)
    return high, middle, rest - middle


def kernel(
    dims,
    counts_s, counts_v, table_ref, z_home_ref, keys_ref, values_ref, w_embed_ref, step_bias_ref,
    gain_ref, w_query_ref, w_out_ref, out_ref,
    zf, kbd, vbd, wr, wo, z_ref, normed, queries, attended, part, send, recv,
    psend, precv, fsend, frecv,
):
    nodes, tensors, groups, halves, steps, smax, pdev = dims
    me = lax.axis_index("pocket")
    mt = lax.axis_index("tensor")
    width = w_embed_ref.shape[1]
    channels = w_embed_ref.shape[0]
    atoms = z_home_ref.shape[2] // channels
    local = w_query_ref.shape[0]
    pairs = local // (2 * HEAD)
    rows = GS * atoms
    per = smax // GS
    pockets = nodes * pdev

    barrier = pltpu.get_barrier_semaphore()
    for k in range(1, nodes):
        pl.semaphore_signal(barrier, 1, device_id=(lax.rem(me + k, nodes), mt), device_id_type=pl.DeviceIdType.MESH)
    for k in range(1, tensors):
        pl.semaphore_signal(barrier, 1, device_id=(me, lax.rem(mt + k, tensors)), device_id_type=pl.DeviceIdType.MESH)

    tops = []
    total = 0
    for p in range(pdev):
        total = total + (counts_s[me * pdev + p] + (GS - 1)) // GS
        tops.append(total)

    def place(g):
        pocket = jnp.int32(0)
        first = jnp.int32(0)
        for p in range(pdev - 1):
            past = g >= tops[p]
            pocket = jnp.where(past, p + 1, pocket)
            first = jnp.where(past, tops[p], first)
        block = jnp.clip(g - first, 0, per - 1)
        return pocket, pocket * per + block

    w_full = w_embed_ref[...]
    w_mid = w_full - jnp.mean(w_full, axis=1, keepdims=True)
    a, b, c = split3(w_mid)
    w_six = [v.astype(BF16) for v in (a, b, c, a, b, a)]
    bias = step_bias_ref[...]
    bias = bias - jnp.mean(bias, axis=1, keepdims=True)
    ba, bb, bc = split3(bias)
    row_id = iota((channels, width), 0)
    for t in range(steps):
        for k in range(6):
            wr[t, k * channels:(k + 1) * channels, :] = w_six[k]
        block = jnp.where(row_id == 0, ba[t:t + 1], jnp.where(row_id == 1, bb[t:t + 1], jnp.where(row_id == 2, bc[t:t + 1], 0.0)))
        wr[t, 6 * channels:7 * channels, :] = block.astype(BF16)
        wr[t, 7 * channels:, :] = jnp.zeros((128 - 7 * channels, width), BF16)
    spread = (iota((channels, 128), 0) == lax.rem(iota((channels, 128), 1), channels)).astype(BF16)
    wo[...] = jnp.dot(w_out_ref[...], spread, preferred_element_type=F32).astype(BF16)

    residues = keys_ref.shape[2]
    top = iota((2 * HEAD, residues), 0) < HEAD
    ones = (
        (iota((2 * residues, 2 * HEAD), 0) < residues) == (iota((2 * residues, 2 * HEAD), 1) < HEAD)
    ).astype(F32).astype(BF16)

    def prepare(i, carry):
        p = i // pairs
        hp = lax.rem(i, pairs)
        start = pl.multiple_of(hp * 2 * HEAD, 2 * HEAD)
        k_pair = keys_ref[p, pl.ds(start, 2 * HEAD), :].astype(F32) * 0.125
        kbd[i, :, :residues] = jnp.where(top, k_pair, 0.0).astype(BF16)
        kbd[i, :, residues:] = jnp.where(top, 0.0, k_pair).astype(BF16)
        v_pair = values_ref[p, pl.ds(start, 2 * HEAD), :].astype(F32)
        vbd[i, :residues, :2 * HEAD] = jnp.where(top, v_pair, 0.0).T.astype(BF16)
        vbd[i, residues:, :2 * HEAD] = jnp.where(top, 0.0, v_pair).T.astype(BF16)
        vbd[i, :, 2 * HEAD:] = ones
        return carry

    lax.fori_loop(0, pdev * pairs, prepare, 0)

    for p in range(pdev):
        block = z_home_ref[p].astype(F32)
        for j in range(per):
            zf[p * per + j] = block[j * GS:(j + 1) * GS]

    flat = atoms * channels
    own_atom = iota((rows, flat), 1) // channels == lax.rem(iota((rows, flat), 0), atoms)
    fold = (lax.rem(iota((flat, 128), 0), channels) == lax.rem(iota((flat, 128), 1), channels)).astype(BF16)
    for g in range(groups):
        pocket, block = place(jnp.int32(g))
        flat_z = zf[block]
        copies = jnp.broadcast_to(flat_z[:, None, :], (GS, atoms, flat)).reshape(rows, flat)
        copies = jnp.where(own_atom, copies, 0.0).astype(BF16)
        z_ref[g * rows:(g + 1) * rows, :] = jnp.dot(copies, fold, preferred_element_type=F32)

    pl.semaphore_wait(barrier, nodes + tensors - 2)

    lane = iota((rows, 128), 1)
    gain = gain_ref[...]

    def exchange(t, h, k):
        first, count = halves[h]
        here = part.at[t, mt, first * rows:(first + count) * rows, :]
        return pltpu.make_async_remote_copy(
            src_ref=here, dst_ref=here, send_sem=psend.at[t, h, k - 1], recv_sem=precv.at[t, h, k - 1],
            device_id=(me, lax.rem(mt + k, tensors)), device_id_type=pl.DeviceIdType.MESH,
        )

    def pick(t, table):
        value = jnp.float32(table[-1])
        for k in range(steps - 1):
            value = jnp.where(t == k, jnp.float32(table[k]), value)
        return value

    keeps = [0.95 + 0.01 * k for k in range(steps)]
    pushes = [-0.8 + 0.1 * k for k in range(steps)]

    def update(t, h):
        first, count = halves[h]
        for k in range(1, tensors):
            exchange(t, h, k).wait()
        window = slice(first * rows, (first + count) * rows)
        guess = part[t, 0, window, :]
        for k in range(1, tensors):
            guess = guess + part[t, k, window, :]
        z_ref[window, :] = pick(t, keeps) * z_ref[window, :] + pick(t, pushes) * guess

    def compute(t, h):
        first, count = halves[h]

        def embed(i, carry):
            start = pl.multiple_of((first + i) * rows, rows)
            high, middle, low = split3(z_ref[pl.ds(start, rows), :])
            left = jnp.where(lane < 3 * channels, high, jnp.where(lane < 5 * channels, middle, jnp.where(lane < 6 * channels, low, 1.0)))
            centred = jnp.dot(left.astype(BF16), wr[t], preferred_element_type=F32)
            variance = jnp.sum(centred * centred, axis=1, keepdims=True) * (1.0 / width)
            normed[pl.ds(start, rows), :] = (centred * lax.rsqrt(variance + EPS) * gain).astype(BF16)
            return carry

        lax.fori_loop(0, count, embed, 0)
        window = slice(first * rows, (first + count) * rows)
        queries[window, :] = lax.dot_general(
            normed[window, :], w_query_ref[...], NT, preferred_element_type=F32
        ).astype(BF16)

        def attend(i, carry):
            g = first + i
            start = pl.multiple_of(g * rows, rows)
            pocket, _ = place(g)
            for hp in range(pairs):
                cols = slice(hp * 2 * HEAD, (hp + 1) * 2 * HEAD)
                scores = jnp.dot(queries[pl.ds(start, rows), cols], kbd[pocket * pairs + hp], preferred_element_type=F32)
                s0 = scores[:, :residues]
                s1 = scores[:, residues:]
                e0 = jnp.exp(s0 - jnp.max(s0, axis=1, keepdims=True))
                e1 = jnp.exp(s1 - jnp.max(s1, axis=1, keepdims=True))
                e = jnp.concatenate([e0.astype(BF16), e1.astype(BF16)], axis=1)
                mixed = jnp.dot(e, vbd[pocket * pairs + hp], preferred_element_type=F32)
                attended[pl.ds(start, rows), cols] = (mixed[:, :2 * HEAD] / mixed[:, 2 * HEAD:]).astype(BF16)
            return carry

        lax.fori_loop(0, count, attend, 0)
        part[t, mt, window, :] = jnp.dot(attended[window, :], wo[...], preferred_element_type=F32)
        for k in range(1, tensors):
            exchange(t, h, k).start()

    for h in range(len(halves)):
        compute(0, h)

    def step(t, carry):
        for h in range(len(halves)):
            update(t - 1, h)
            compute(t, h)
        return carry

    lax.fori_loop(1, steps, step, 0)

    seats = groups * GS
    slots = -(-WORK // 8) * 8
    lanes = iota((1, seats), 1)
    entry = jnp.full((1, seats), -1, jnp.int32)
    for g in range(groups):
        _, block = place(jnp.int32(g))
        inside = (lanes >= g * GS) & (lanes < (g + 1) * GS) & (g < tops[-1])
        entry = jnp.where(inside, block * GS + lanes - g * GS, entry)
    keep_rows = jnp.zeros((slots, seats), F32)
    send_rows = jnp.zeros((nodes, seats), F32)
    for p in range(pdev):
        target = table_ref[pl.ds(me * pdev + p, 1), :]
        alive = iota((1, smax), 1) < counts_s[me * pdev + p]
        target = jnp.where(alive, target, -1)
        matches = (iota((smax, seats), 0) + p * smax == entry).astype(F32)
        stay = (iota((slots, smax), 0) == target - me * WORK) & (iota((slots, smax), 0) < WORK)
        keep_rows = keep_rows + jnp.dot(stay.astype(F32), matches, preferred_element_type=F32)
        node = iota((nodes, smax), 0)
        leave = (target >= node * WORK) & (target < node * WORK + WORK) & (node != me)
        send_rows = send_rows + jnp.dot(leave.astype(F32), matches, preferred_element_type=F32)
    diagonal = iota((pockets, pockets), 0) == iota((pockets, pockets), 1)
    count_rows = jnp.sum(jnp.where(diagonal, counts_v[...].astype(F32), 0.0), axis=1, keepdims=True)
    here = table_ref[...] - me * WORK
    whose = iota((pockets, smax), 0)
    arrives = (
        (iota((pockets, smax), 1).astype(F32) < count_rows)
        & (here >= 0) & (here < WORK)
        & ((whose < me * pdev) | (whose >= me * pdev + pdev))
    )
    arrival = jnp.max(jnp.where(arrives, here.astype(F32), -1.0), axis=1, keepdims=True)
    by_pocket = (arrival == iota((pockets, slots), 1).astype(F32)).astype(F32)
    pocket_id = iota((pockets, nodes), 0)
    node_id = iota((pockets, nodes), 1) * pdev
    by_node = ((pocket_id >= node_id) & (pocket_id < node_id + pdev)).astype(F32)
    take_rows = lax.dot_general(by_pocket, by_node, TN, preferred_element_type=F32)

    for h in range(len(halves)):
        update(steps - 1, h)
    done = []
    for g in range(groups):
        z = z_ref[g * rows:(g + 1) * rows, :]
        wide = jnp.concatenate([z] * (flat // 128), axis=1)
        done.append(jnp.sum(jnp.where(own_atom, wide, 0.0).reshape(GS, atoms, flat), axis=1))
    done = jnp.concatenate(done, axis=0)
    leaving = jnp.dot(send_rows, done, precision=HIGHEST, preferred_element_type=F32)
    for d in range(nodes):
        send[d] = leaving[d:d + 1]

    def hand(k):
        peer = lax.rem(me + k, nodes)
        return pltpu.make_async_remote_copy(
            src_ref=send.at[peer], dst_ref=recv.at[me], send_sem=fsend.at[k - 1], recv_sem=frecv.at[k - 1],
            device_id=(peer, mt), device_id_type=pl.DeviceIdType.MESH,
        )

    for k in range(1, nodes):
        hand(k).start()
    recv[me] = jnp.zeros((1, flat), F32)
    result = jnp.dot(keep_rows, done, precision=HIGHEST, preferred_element_type=F32)
    for k in range(1, nodes):
        hand(k).wait()
    landed = recv[...].reshape(nodes, flat)
    result = result + jnp.dot(take_rows, landed, precision=HIGHEST, preferred_element_type=F32)
    out_ref[...] = result[:WORK]


def per_device(z_home, counts, table, keys, values, w_embed, step_bias, ln_gain, w_query, w_out):
    nodes = lax.axis_size("pocket")
    tensors = lax.axis_size("tensor")
    pdev, smax, flat = z_home.shape
    channels, width = w_embed.shape
    atoms = flat // channels
    steps = step_bias.shape[0]
    local = w_query.shape[0]
    pairs = local // (2 * HEAD)
    residues = keys.shape[2]
    heavy = WORK + CAP * nodes // 2
    light = WORK - CAP * nodes // 2
    groups = max(
        smax // GS + (heavy - smax + (pdev - 1) * (GS - 1)) // GS,
        (light + pdev * (GS - 1)) // GS,
    )
    rows = GS * atoms
    front = (groups + 1) // 2
    halves = ((0, front), (front, groups - front))
    dims = (nodes, tensors, groups, halves, steps, smax, pdev)
    vmem = pl.BlockSpec(memory_space=pltpu.VMEM)
    smem = pl.BlockSpec(memory_space=pltpu.SMEM)
    return pl.pallas_call(
        functools.partial(kernel, dims),
        out_shape=jax.ShapeDtypeStruct((WORK, flat), F32),
        in_specs=[smem] + [vmem] * 10,
        out_specs=vmem,
        scratch_shapes=[
            pltpu.VMEM((pdev * smax // GS, GS, flat), F32),
            pltpu.VMEM((pdev * pairs, 2 * HEAD, 2 * residues), BF16),
            pltpu.VMEM((pdev * pairs, 2 * residues, 4 * HEAD), BF16),
            pltpu.VMEM((steps, 128, width), BF16),
            pltpu.VMEM((local, 128), BF16),
            pltpu.VMEM((groups * rows, 128), F32),
            pltpu.VMEM((groups * rows, width), BF16),
            pltpu.VMEM((groups * rows, local), BF16),
            pltpu.VMEM((groups * rows, local), BF16),
            pltpu.VMEM((steps, tensors, groups * rows, 128), F32),
            pltpu.VMEM((nodes, 1, flat), F32),
            pltpu.VMEM((nodes, 1, flat), F32),
            pltpu.SemaphoreType.DMA((steps, 2, max(tensors - 1, 1))),
            pltpu.SemaphoreType.DMA((steps, 2, max(tensors - 1, 1))),
            pltpu.SemaphoreType.DMA((nodes - 1,)),
            pltpu.SemaphoreType.DMA((nodes - 1,)),
        ],
        compiler_params=pltpu.CompilerParams(
            collective_id=0, has_side_effects=True, vmem_limit_bytes=60 * 1024 * 1024
        ),
        name="denoise",
    )(
        counts, counts.reshape(1, -1), table, z_home, keys, values, w_embed, step_bias,
        ln_gain.reshape(1, -1), w_query, w_out,
    )


def solution(mesh):
    return jax.shard_map(
        per_device,
        mesh=mesh,
        in_specs=(
            P("pocket", None, None),
            P(),
            P(),
            P("pocket", "tensor", None),
            P("pocket", "tensor", None),
            P(),
            P(),
            P(),
            P("tensor", None),
            P("tensor", None),
        ),
        out_specs=P("pocket", None),
        check_vma=False,
    )
```

```python
import functools

import jax
import jax.numpy as jnp
from jax import lax
from jax.experimental import pallas as pl
from jax.experimental.pallas import tpu as pltpu
from jax.sharding import PartitionSpec as P

HEAD = 64
CAP = 1
WORK = 36
GS = 8
EPS = 1e-05
F32 = jnp.float32
BF16 = jnp.bfloat16
HIGHEST = lax.Precision.HIGHEST
NT = (((1,), (1,)), ((), ()))
TN = (((0,), (0,)), ((), ()))


def iota(shape, axis):
    return lax.broadcasted_iota(jnp.int32, shape, axis)


def split3(value):
    high = value.astype(BF16).astype(F32)
    rest = value - high
    middle = rest.astype(BF16).astype(F32)
    return high, middle, rest - middle


def kernel(
    dims,
    counts_s, counts_v, table_ref, z_home_ref, keys_hbm, values_hbm, w_embed_ref, step_bias_ref,
    gain_ref, w_query_hbm, w_out_ref, out_ref,
    keys_ref, values_ref, w_query_ref, load, table_s, zf, kbd, vbd, wr, wo, z_ref, normed, queries, attended, part, send, recv,
    psend, precv, fsend, frecv,
):
    nodes, tensors, groups, halves, steps, smax, pdev = dims
    me = lax.axis_index("pocket")
    mt = lax.axis_index("tensor")
    width = w_embed_ref.shape[1]
    channels = w_embed_ref.shape[0]
    atoms = z_home_ref.shape[2] // channels
    local = w_query_ref.shape[0]
    pairs = local // (2 * HEAD)
    rows = GS * atoms
    per = smax // GS
    pockets = nodes * pdev

    barrier = pltpu.get_barrier_semaphore()
    for k in range(1, nodes):
        pl.semaphore_signal(barrier, 1, device_id=(lax.rem(me + k, nodes), mt), device_id_type=pl.DeviceIdType.MESH)
    for k in range(1, tensors):
        pl.semaphore_signal(barrier, 1, device_id=(me, lax.rem(mt + k, tensors)), device_id_type=pl.DeviceIdType.MESH)

    loads = [
        pltpu.make_async_copy(source, target, load.at[k])
        for k, (source, target) in enumerate(
            ((keys_hbm, keys_ref), (values_hbm, values_ref), (w_query_hbm, w_query_ref))
        )
    ]
    for copy in loads:
        copy.start()

    tops = []
    total = 0
    for p in range(pdev):
        total = total + (counts_s[me * pdev + p] + (GS - 1)) // GS
        tops.append(total)

    def place(g):
        pocket = jnp.int32(0)
        first = jnp.int32(0)
        for p in range(pdev - 1):
            past = g >= tops[p]
            pocket = jnp.where(past, p + 1, pocket)
            first = jnp.where(past, tops[p], first)
        block = jnp.clip(g - first, 0, per - 1)
        return pocket, pocket * per + block

    w_full = w_embed_ref[...]
    w_mid = w_full - jnp.mean(w_full, axis=1, keepdims=True)
    a, b, c = split3(w_mid)
    w_six = [v.astype(BF16) for v in (a, b, c, a, b, a)]
    bias = step_bias_ref[...]
    bias = bias - jnp.mean(bias, axis=1, keepdims=True)
    ba, bb, bc = split3(bias)
    row_id = iota((channels, width), 0)
    for t in range(steps):
        for k in range(6):
            wr[t, k * channels:(k + 1) * channels, :] = w_six[k]
        block = jnp.where(row_id == 0, ba[t:t + 1], jnp.where(row_id == 1, bb[t:t + 1], jnp.where(row_id == 2, bc[t:t + 1], 0.0)))
        wr[t, 6 * channels:7 * channels, :] = block.astype(BF16)
        wr[t, 7 * channels:, :] = jnp.zeros((128 - 7 * channels, width), BF16)
    spread = (iota((channels, 128), 0) == lax.rem(iota((channels, 128), 1), channels)).astype(BF16)
    wo[...] = lax.dot_general(spread, w_out_ref[...], TN, preferred_element_type=F32).astype(BF16)

    residues = keys_ref.shape[2]
    zeros = jnp.zeros((HEAD, residues), BF16)
    ones = jnp.ones((HEAD, residues), BF16)
    for p in range(pdev):
        block = z_home_ref[p].astype(F32)
        for j in range(per):
            zf[p * per + j] = block[j * GS:(j + 1) * GS]

    flat = atoms * channels
    own_atom = iota((rows, flat), 1) // channels == lax.rem(iota((rows, flat), 0), atoms)
    fold = (lax.rem(iota((flat, 128), 0), channels) == lax.rem(iota((flat, 128), 1), channels)).astype(BF16)
    for g in range(groups):
        pocket, block = place(jnp.int32(g))
        flat_z = zf[block]
        copies = jnp.broadcast_to(flat_z[:, None, :], (GS, atoms, flat)).reshape(rows, flat)
        copies = jnp.where(own_atom, copies, 0.0).astype(BF16)
        z_ref[g * rows:(g + 1) * rows, :] = jnp.dot(copies, fold, preferred_element_type=F32)

    table_s[...] = table_ref[...].astype(F32).T.astype(jnp.int32)
    seats = groups * GS
    slots = -(-WORK // 8) * 8
    lanes = iota((1, seats), 1)
    entry = jnp.full((1, seats), -1, jnp.int32)
    for g in range(groups):
        _, block = place(jnp.int32(g))
        inside = (lanes >= g * GS) & (lanes < (g + 1) * GS) & (g < tops[-1])
        entry = jnp.where(inside, block * GS + lanes - g * GS, entry)
    keep_rows = jnp.zeros((slots, seats), F32)
    send_rows = jnp.zeros((nodes, seats), F32)
    for p in range(pdev):
        target = table_s[pl.ds(me * pdev + p, 1), :]
        alive = iota((1, smax), 1) < counts_s[me * pdev + p]
        target = jnp.where(alive, target, -1)
        matches = (iota((smax, seats), 0) + p * smax == entry).astype(F32)
        stay = (iota((slots, smax), 0) == target - me * WORK) & (iota((slots, smax), 0) < WORK)
        keep_rows = keep_rows + jnp.dot(stay.astype(F32), matches, preferred_element_type=F32)
        node = iota((nodes, smax), 0)
        leave = (target >= node * WORK) & (target < node * WORK + WORK) & (node != me)
        send_rows = send_rows + jnp.dot(leave.astype(F32), matches, preferred_element_type=F32)
    diagonal = iota((pockets, pockets), 0) == iota((pockets, pockets), 1)
    count_rows = jnp.sum(jnp.where(diagonal, counts_v[...].astype(F32), 0.0), axis=1, keepdims=True)
    here = table_s[...] - me * WORK
    whose = iota((pockets, smax), 0)
    arrives = (
        (iota((pockets, smax), 1).astype(F32) < count_rows)
        & (here >= 0) & (here < WORK)
        & ((whose < me * pdev) | (whose >= me * pdev + pdev))
    )
    arrival = jnp.max(jnp.where(arrives, here.astype(F32), -1.0), axis=1, keepdims=True)
    by_pocket = (arrival == iota((pockets, slots), 1).astype(F32)).astype(F32)
    pocket_id = iota((pockets, nodes), 0)
    node_id = iota((pockets, nodes), 1) * pdev
    by_node = ((pocket_id >= node_id) & (pocket_id < node_id + pdev)).astype(F32)
    take_rows = lax.dot_general(by_pocket, by_node, TN, preferred_element_type=F32)

    loads[0].wait()
    loads[1].wait()
    for p in range(pdev):
        for hp in range(pairs):
            i = p * pairs + hp
            for side in range(2):
                inner = slice(side * HEAD, (side + 1) * HEAD)
                outer = slice(hp * 2 * HEAD + side * HEAD, hp * 2 * HEAD + (side + 1) * HEAD)
                mine = slice(side * residues, (side + 1) * residues)
                other = slice((1 - side) * residues, (2 - side) * residues)
                kbd[i, inner, mine] = keys_ref[p, outer, :] * jnp.asarray(0.125, BF16)
                kbd[i, inner, other] = zeros
                vbd[i, inner, mine] = values_ref[p, outer, :]
                vbd[i, inner, other] = zeros
                below = slice(2 * HEAD + side * HEAD, 2 * HEAD + (side + 1) * HEAD)
                vbd[i, below, mine] = ones
                vbd[i, below, other] = zeros

    loads[2].wait()
    pl.semaphore_wait(barrier, nodes + tensors - 2)

    lane = iota((rows, 128), 1)
    gain = gain_ref[...].reshape(1, width)

    def exchange(t, h, k):
        first, count = halves[h]
        here = part.at[t, mt, first * rows:(first + count) * rows, :]
        return pltpu.make_async_remote_copy(
            src_ref=here, dst_ref=here, send_sem=psend.at[t, h, k - 1], recv_sem=precv.at[t, h, k - 1],
            device_id=(me, lax.rem(mt + k, tensors)), device_id_type=pl.DeviceIdType.MESH,
        )

    def pick(t, table):
        value = jnp.float32(table[-1])
        for k in range(steps - 1):
            value = jnp.where(t == k, jnp.float32(table[k]), value)
        return value

    keeps = [0.95 + 0.01 * k for k in range(steps)]
    pushes = [-0.8 + 0.1 * k for k in range(steps)]

    def update(t, h):
        first, count = halves[h]
        for k in range(1, tensors):
            exchange(t, h, k).wait()
        window = slice(first * rows, (first + count) * rows)
        guess = part[t, 0, window, :]
        for k in range(1, tensors):
            guess = guess + part[t, k, window, :]
        z_ref[window, :] = pick(t, keeps) * z_ref[window, :] + pick(t, pushes) * guess

    def compute(t, h):
        first, count = halves[h]

        def embed(i):
            start = (first + i) * rows
            high, middle, low = split3(z_ref[pl.ds(start, rows), :])
            left = jnp.where(lane < 3 * channels, high, jnp.where(lane < 5 * channels, middle, jnp.where(lane < 6 * channels, low, 1.0)))
            centred = jnp.dot(left.astype(BF16), wr[t], preferred_element_type=F32)
            variance = jnp.sum(centred * centred, axis=1, keepdims=True) * (1.0 / width)
            normed[pl.ds(start, rows), :] = (centred * lax.rsqrt(variance + EPS) * gain).astype(BF16)

        for i in range(count):
            embed(i)
        window = slice(first * rows, (first + count) * rows)
        queries[window, :] = lax.dot_general(
            normed[window, :], w_query_ref[...], NT, preferred_element_type=F32
        ).astype(BF16)

        def attend(i):
            g = first + i
            start = g * rows
            pocket, _ = place(g)
            for hp in range(pairs):
                cols = slice(hp * 2 * HEAD, (hp + 1) * 2 * HEAD)
                scores = jnp.dot(queries[pl.ds(start, rows), cols], kbd[pocket * pairs + hp], preferred_element_type=F32)
                s0 = scores[:, :residues]
                s1 = scores[:, residues:]
                e0 = jnp.exp(s0 - jnp.max(s0, axis=1, keepdims=True))
                e1 = jnp.exp(s1 - jnp.max(s1, axis=1, keepdims=True))
                e = jnp.concatenate([e0.astype(BF16), e1.astype(BF16)], axis=1)
                mixed = lax.dot_general(e, vbd[pocket * pairs + hp], NT, preferred_element_type=F32)
                attended[pl.ds(start, rows), cols] = (mixed[:, :2 * HEAD] / mixed[:, 2 * HEAD:]).astype(BF16)

        for i in range(count):
            attend(i)
        part[t, mt, window, :] = lax.dot_general(attended[window, :], wo[...], NT, preferred_element_type=F32)
        for k in range(1, tensors):
            exchange(t, h, k).start()

    for h in range(len(halves)):
        compute(0, h)

    def step(t, carry):
        for h in range(len(halves)):
            update(t - 1, h)
            compute(t, h)
        return carry

    lax.fori_loop(1, steps, step, 0)

    for h in range(len(halves)):
        update(steps - 1, h)
    done = []
    for g in range(groups):
        z = z_ref[g * rows:(g + 1) * rows, :]
        wide = jnp.concatenate([z] * (flat // 128), axis=1)
        done.append(jnp.sum(jnp.where(own_atom, wide, 0.0).reshape(GS, atoms, flat), axis=1))
    done = jnp.concatenate(done, axis=0)
    leaving = jnp.dot(send_rows, done, precision=HIGHEST, preferred_element_type=F32)
    for d in range(nodes):
        send[d] = leaving[d:d + 1]

    def hand(k):
        peer = lax.rem(me + k, nodes)
        return pltpu.make_async_remote_copy(
            src_ref=send.at[peer], dst_ref=recv.at[me], send_sem=fsend.at[k - 1], recv_sem=frecv.at[k - 1],
            device_id=(peer, mt), device_id_type=pl.DeviceIdType.MESH,
        )

    for k in range(1, nodes):
        hand(k).start()
    recv[me] = jnp.zeros((1, flat), F32)
    result = jnp.dot(keep_rows, done, precision=HIGHEST, preferred_element_type=F32)
    for k in range(1, nodes):
        hand(k).wait()
    landed = recv[...].reshape(nodes, flat)
    result = result + jnp.dot(take_rows, landed, precision=HIGHEST, preferred_element_type=F32)
    out_ref[...] = result[:WORK]


def per_device(z_home, counts, table, keys, values, w_embed, step_bias, ln_gain, w_query, w_out):
    nodes = lax.axis_size("pocket")
    tensors = lax.axis_size("tensor")
    pdev, smax, flat = z_home.shape
    channels, width = w_embed.shape
    atoms = flat // channels
    steps = step_bias.shape[0]
    local = w_query.shape[0]
    pairs = local // (2 * HEAD)
    residues = keys.shape[2]
    heavy = WORK + CAP * nodes // 2
    light = WORK - CAP * nodes // 2
    groups = max(
        smax // GS + (heavy - smax + (pdev - 1) * (GS - 1)) // GS,
        (light + pdev * (GS - 1)) // GS,
    )
    rows = GS * atoms
    front = (groups + 1) // 2
    halves = ((0, front), (front, groups - front))
    dims = (nodes, tensors, groups, halves, steps, smax, pdev)
    vmem = pl.BlockSpec(memory_space=pltpu.VMEM)
    smem = pl.BlockSpec(memory_space=pltpu.SMEM)
    hbm = pl.BlockSpec(memory_space=pl.ANY)
    return pl.pallas_call(
        functools.partial(kernel, dims),
        out_shape=jax.ShapeDtypeStruct((WORK, flat), F32),
        in_specs=[smem] + [vmem] * 3 + [hbm] * 2 + [vmem] * 3 + [hbm, vmem],
        out_specs=vmem,
        scratch_shapes=[
            pltpu.VMEM(keys.shape, BF16),
            pltpu.VMEM(values.shape, BF16),
            pltpu.VMEM(w_query.shape, BF16),
            pltpu.SemaphoreType.DMA((3,)),
            pltpu.VMEM(table.shape, jnp.int32),
            pltpu.VMEM((pdev * smax // GS, GS, flat), F32),
            pltpu.VMEM((pdev * pairs, 2 * HEAD, 2 * residues), BF16),
            pltpu.VMEM((pdev * pairs, 4 * HEAD, 2 * residues), BF16),
            pltpu.VMEM((steps, 128, width), BF16),
            pltpu.VMEM((128, local), BF16),
            pltpu.VMEM((groups * rows, 128), F32),
            pltpu.VMEM((groups * rows, width), BF16),
            pltpu.VMEM((groups * rows, local), BF16),
            pltpu.VMEM((groups * rows, local), BF16),
            pltpu.VMEM((steps, tensors, groups * rows, 128), F32),
            pltpu.VMEM((nodes, 1, flat), F32),
            pltpu.VMEM((nodes, 1, flat), F32),
            pltpu.SemaphoreType.DMA((steps, 2, max(tensors - 1, 1))),
            pltpu.SemaphoreType.DMA((steps, 2, max(tensors - 1, 1))),
            pltpu.SemaphoreType.DMA((nodes - 1,)),
            pltpu.SemaphoreType.DMA((nodes - 1,)),
        ],
        compiler_params=pltpu.CompilerParams(
            collective_id=0, has_side_effects=True, vmem_limit_bytes=60 * 1024 * 1024
        ),
        name="denoise",
    )(
        counts, counts.reshape(1, -1), table.T, z_home, keys, values, w_embed, step_bias,
        ln_gain, w_query, w_out.T,
    )


def solution(mesh):
    return jax.shard_map(
        per_device,
        mesh=mesh,
        in_specs=(
            P("pocket", None, None),
            P(),
            P(),
            P("pocket", "tensor", None),
            P("pocket", "tensor", None),
            P(),
            P(),
            P(),
            P("tensor", None),
            P("tensor", None),
        ),
        out_specs=P("pocket", None),
        check_vma=False,
    )
```

```python
import functools

import jax
import jax.numpy as jnp
from jax import lax
from jax.experimental import pallas as pl
from jax.experimental.pallas import tpu as pltpu
from jax.sharding import PartitionSpec as P

HEAD = 64
CAP = 1
WORK = 36
GS = 8
EPS = 1e-05
F32 = jnp.float32
BF16 = jnp.bfloat16
HIGHEST = lax.Precision.HIGHEST
NT = (((1,), (1,)), ((), ()))
TN = (((0,), (0,)), ((), ()))


def iota(shape, axis):
    return lax.broadcasted_iota(jnp.int32, shape, axis)


def split3(value):
    high = value.astype(BF16).astype(F32)
    rest = value - high
    middle = rest.astype(BF16).astype(F32)
    return high, middle, rest - middle


def kernel(
    dims,
    counts_s, counts_v, table_ref, z_home_ref, keys_hbm, values_hbm, w_embed_ref, step_bias_ref,
    gain_ref, w_query_hbm, w_out_ref, out_ref,
    keys_ref, values_ref, w_query_ref, load, table_s, zf, kbd, vbd, wr, gains, z_ref, normed, queries, attended, part, send, recv,
    psend, precv, fsend, frecv,
):
    nodes, tensors, groups, halves, steps, smax, pdev = dims
    me = lax.axis_index("pocket")
    mt = lax.axis_index("tensor")
    width = w_embed_ref.shape[1]
    channels = w_embed_ref.shape[0]
    atoms = z_home_ref.shape[2] // channels
    local = w_query_ref.shape[0]
    pairs = local // (2 * HEAD)
    rows = GS * atoms
    per = smax // GS
    pockets = nodes * pdev

    barrier = pltpu.get_barrier_semaphore()
    for k in range(1, nodes):
        pl.semaphore_signal(barrier, 1, device_id=(lax.rem(me + k, nodes), mt), device_id_type=pl.DeviceIdType.MESH)
    for k in range(1, tensors):
        pl.semaphore_signal(barrier, 1, device_id=(me, lax.rem(mt + k, tensors)), device_id_type=pl.DeviceIdType.MESH)

    loads = [
        pltpu.make_async_copy(source, target, load.at[k])
        for k, (source, target) in enumerate(
            ((keys_hbm, keys_ref), (values_hbm, values_ref), (w_query_hbm, w_query_ref))
        )
    ]
    for copy in loads:
        copy.start()

    tops = []
    total = 0
    for p in range(pdev):
        total = total + (counts_s[me * pdev + p] + (GS - 1)) // GS
        tops.append(total)

    def place(g):
        pocket = jnp.int32(0)
        first = jnp.int32(0)
        for p in range(pdev - 1):
            past = g >= tops[p]
            pocket = jnp.where(past, p + 1, pocket)
            first = jnp.where(past, tops[p], first)
        block = jnp.clip(g - first, 0, per - 1)
        return pocket, pocket * per + block

    w_full = w_embed_ref[...]
    w_mid = w_full - jnp.mean(w_full, axis=1, keepdims=True)
    a, b, c = split3(w_mid)
    ba, bb, bc = split3(step_bias_ref[...] - jnp.mean(step_bias_ref[...], axis=1, keepdims=True))
    padding = jnp.zeros((128 - 6 * channels - 3 * steps, width), F32)
    stacked = jnp.concatenate([a, b, c, a, b, a, ba, bb, bc, padding], axis=0)
    wr[...] = stacked.T.astype(BF16)
    gains[...] = jnp.broadcast_to(gain_ref[...].reshape(1, width), (128, width)).T

    residues = keys_ref.shape[2]
    zeros = jnp.zeros((HEAD, residues), BF16)
    left_head = iota((residues, 2 * HEAD), 1) < HEAD
    for p in range(pdev):
        block = z_home_ref[p].astype(F32)
        for j in range(per):
            zf[p * per + j] = block[j * GS:(j + 1) * GS]

    flat = atoms * channels
    own_atom = iota((rows, flat), 1) // channels == lax.rem(iota((rows, flat), 0), atoms)
    fold = (lax.rem(iota((channels, flat), 1), channels) == iota((channels, flat), 0)).astype(F32)
    for g in range(groups):
        pocket, block = place(jnp.int32(g))
        flat_z = zf[block]
        copies = jnp.broadcast_to(flat_z[:, None, :], (GS, atoms, flat)).reshape(rows, flat)
        copies = jnp.where(own_atom, copies, 0.0).astype(BF16)
        z_ref[:, g * rows:(g + 1) * rows] = lax.dot_general(fold.astype(BF16), copies, NT, preferred_element_type=F32)

    table_s[...] = table_ref[...].astype(F32).T.astype(jnp.int32)
    seats = groups * GS
    slots = -(-WORK // 8) * 8
    lanes = iota((1, seats), 1)
    entry = jnp.full((1, seats), -1, jnp.int32)
    for g in range(groups):
        _, block = place(jnp.int32(g))
        inside = (lanes >= g * GS) & (lanes < (g + 1) * GS) & (g < tops[-1])
        entry = jnp.where(inside, block * GS + lanes - g * GS, entry)
    keep_rows = jnp.zeros((slots, seats), F32)
    send_rows = jnp.zeros((nodes, seats), F32)
    for p in range(pdev):
        target = table_s[pl.ds(me * pdev + p, 1), :]
        alive = iota((1, smax), 1) < counts_s[me * pdev + p]
        target = jnp.where(alive, target, -1)
        matches = (iota((smax, seats), 0) + p * smax == entry).astype(F32)
        stay = (iota((slots, smax), 0) == target - me * WORK) & (iota((slots, smax), 0) < WORK)
        keep_rows = keep_rows + jnp.dot(stay.astype(F32), matches, preferred_element_type=F32)
        node = iota((nodes, smax), 0)
        leave = (target >= node * WORK) & (target < node * WORK + WORK) & (node != me)
        send_rows = send_rows + jnp.dot(leave.astype(F32), matches, preferred_element_type=F32)
    diagonal = iota((pockets, pockets), 0) == iota((pockets, pockets), 1)
    count_rows = jnp.sum(jnp.where(diagonal, counts_v[...].astype(F32), 0.0), axis=1, keepdims=True)
    here = table_s[...] - me * WORK
    whose = iota((pockets, smax), 0)
    arrives = (
        (iota((pockets, smax), 1).astype(F32) < count_rows)
        & (here >= 0) & (here < WORK)
        & ((whose < me * pdev) | (whose >= me * pdev + pdev))
    )
    arrival = jnp.max(jnp.where(arrives, here.astype(F32), -1.0), axis=1, keepdims=True)
    by_pocket = (arrival == iota((pockets, slots), 1).astype(F32)).astype(F32)
    pocket_id = iota((pockets, nodes), 0)
    node_id = iota((pockets, nodes), 1) * pdev
    by_node = ((pocket_id >= node_id) & (pocket_id < node_id + pdev)).astype(F32)
    take_rows = lax.dot_general(by_pocket, by_node, TN, preferred_element_type=F32)

    loads[0].wait()
    loads[1].wait()
    for p in range(pdev):
        for hp in range(pairs):
            i = p * pairs + hp
            turned = (keys_ref[p, hp * 2 * HEAD:(hp + 1) * 2 * HEAD, :].astype(F32) * 0.125).T
            kbd[i, :residues, :] = jnp.where(left_head, turned, 0.0).astype(BF16)
            kbd[i, residues:, :] = jnp.where(left_head, 0.0, turned).astype(BF16)
            for side in range(2):
                inner = slice(side * HEAD, (side + 1) * HEAD)
                outer = slice(hp * 2 * HEAD + side * HEAD, hp * 2 * HEAD + (side + 1) * HEAD)
                vbd[i, inner, side * residues:(side + 1) * residues] = values_ref[p, outer, :]
                vbd[i, inner, (1 - side) * residues:(2 - side) * residues] = zeros

    loads[2].wait()
    pl.semaphore_wait(barrier, nodes + tensors - 2)


    def exchange(t, h, k):
        first, count = halves[h]
        here = part.at[t, mt, :, first * rows:(first + count) * rows]
        return pltpu.make_async_remote_copy(
            src_ref=here, dst_ref=here, send_sem=psend.at[t, h, k - 1], recv_sem=precv.at[t, h, k - 1],
            device_id=(me, lax.rem(mt + k, tensors)), device_id_type=pl.DeviceIdType.MESH,
        )

    def pick(t, table):
        value = jnp.float32(table[-1])
        for k in range(steps - 1):
            value = jnp.where(t == k, jnp.float32(table[k]), value)
        return value

    keeps = [0.95 + 0.01 * k for k in range(steps)]
    pushes = [-0.8 + 0.1 * k for k in range(steps)]

    def update(t, h):
        first, count = halves[h]
        for k in range(1, tensors):
            exchange(t, h, k).wait()
        window = slice(first * rows, (first + count) * rows)
        guess = part[t, 0, :, window]
        for k in range(1, tensors):
            guess = guess + part[t, k, :, window]
        z_ref[:, window] = pick(t, keeps) * z_ref[:, window] + pick(t, pushes) * guess

    def compute(t, h):
        first, count = halves[h]

        window = slice(first * rows, (first + count) * rows)
        for start in range(first, first + count, 2):
            span = min(2, first + count - start)
            some = slice(start * rows, (start + span) * rows)
            high, middle, low = split3(z_ref[:, some])
            rest_id = iota((128 - 6 * channels, span * rows), 0)
            flags = ((lax.rem(rest_id, steps) == t) & (rest_id < 3 * steps)).astype(F32)
            right = jnp.concatenate([high, high, high, middle, middle, low, flags], axis=0).astype(BF16)
            centred = jnp.dot(wr[...], right, preferred_element_type=F32)
            variance = jnp.sum(centred * centred, axis=0, keepdims=True) * (1.0 / width)
            scale = lax.rsqrt(variance + EPS)
            for k in range(span):
                part_k = slice(k * rows, (k + 1) * rows)
                normed[:, (start + k) * rows:(start + k + 1) * rows] = (
                    centred[:, part_k] * scale[:, part_k] * gains[...]
                ).astype(BF16)
        queries[:, window] = jnp.dot(w_query_ref[...], normed[:, window], preferred_element_type=F32).astype(BF16)

        for g in range(first, first + count):
            lanes_g = slice(g * rows, (g + 1) * rows)
            pocket, _ = place(jnp.int32(g))
            for hp in range(pairs):
                cols = slice(hp * 2 * HEAD, (hp + 1) * 2 * HEAD)
                scores = jnp.dot(kbd[pocket * pairs + hp], queries[cols, lanes_g], preferred_element_type=F32)
                s0 = scores[:residues]
                s1 = scores[residues:]
                e0 = jnp.exp(s0 - jnp.max(s0, axis=0, keepdims=True))
                e1 = jnp.exp(s1 - jnp.max(s1, axis=0, keepdims=True))
                r0 = 1.0 / jnp.sum(e0, axis=0, keepdims=True)
                r1 = 1.0 / jnp.sum(e1, axis=0, keepdims=True)
                e = jnp.concatenate([e0.astype(BF16), e1.astype(BF16)], axis=0)
                mixed = jnp.dot(vbd[pocket * pairs + hp], e, preferred_element_type=F32)
                attended[hp * 2 * HEAD:hp * 2 * HEAD + HEAD, lanes_g] = (mixed[:HEAD] * r0).astype(BF16)
                attended[hp * 2 * HEAD + HEAD:(hp + 1) * 2 * HEAD, lanes_g] = (mixed[HEAD:] * r1).astype(BF16)
        part[t, mt, :, window] = jnp.dot(w_out_ref[...], attended[:, window], preferred_element_type=F32)
        for k in range(1, tensors):
            exchange(t, h, k).start()

    for h in range(len(halves)):
        compute(0, h)

    def step(t, carry):
        for h in range(len(halves)):
            update(t - 1, h)
            compute(t, h)
        return carry

    lax.fori_loop(1, steps, step, 0)

    for h in range(len(halves)):
        update(steps - 1, h)
    done = []
    for g in range(groups):
        wide = lax.dot_general(
            z_ref[:, g * rows:(g + 1) * rows], fold, TN, precision=HIGHEST, preferred_element_type=F32
        )
        done.append(jnp.sum(jnp.where(own_atom, wide, 0.0).reshape(GS, atoms, flat), axis=1))
    done = jnp.concatenate(done, axis=0)
    leaving = jnp.dot(send_rows, done, precision=HIGHEST, preferred_element_type=F32)
    for d in range(nodes):
        send[d] = leaving[d:d + 1]

    def hand(k):
        peer = lax.rem(me + k, nodes)
        return pltpu.make_async_remote_copy(
            src_ref=send.at[peer], dst_ref=recv.at[me], send_sem=fsend.at[k - 1], recv_sem=frecv.at[k - 1],
            device_id=(peer, mt), device_id_type=pl.DeviceIdType.MESH,
        )

    for k in range(1, nodes):
        hand(k).start()
    recv[me] = jnp.zeros((1, flat), F32)
    result = jnp.dot(keep_rows, done, precision=HIGHEST, preferred_element_type=F32)
    for k in range(1, nodes):
        hand(k).wait()
    landed = recv[...].reshape(nodes, flat)
    result = result + jnp.dot(take_rows, landed, precision=HIGHEST, preferred_element_type=F32)
    out_ref[...] = result[:WORK]


def per_device(z_home, counts, table, keys, values, w_embed, step_bias, ln_gain, w_query, w_out):
    nodes = lax.axis_size("pocket")
    tensors = lax.axis_size("tensor")
    pdev, smax, flat = z_home.shape
    channels, width = w_embed.shape
    atoms = flat // channels
    steps = step_bias.shape[0]
    local = w_query.shape[0]
    pairs = local // (2 * HEAD)
    residues = keys.shape[2]
    heavy = WORK + CAP * nodes // 2
    light = WORK - CAP * nodes // 2
    groups = max(
        smax // GS + (heavy - smax + (pdev - 1) * (GS - 1)) // GS,
        (light + pdev * (GS - 1)) // GS,
    )
    rows = GS * atoms
    front = (groups + 1) // 2
    halves = ((0, front), (front, groups - front))
    dims = (nodes, tensors, groups, halves, steps, smax, pdev)
    vmem = pl.BlockSpec(memory_space=pltpu.VMEM)
    smem = pl.BlockSpec(memory_space=pltpu.SMEM)
    hbm = pl.BlockSpec(memory_space=pl.ANY)
    return pl.pallas_call(
        functools.partial(kernel, dims),
        out_shape=jax.ShapeDtypeStruct((WORK, flat), F32),
        in_specs=[smem] + [vmem] * 3 + [hbm] * 2 + [vmem] * 3 + [hbm, vmem],
        out_specs=vmem,
        scratch_shapes=[
            pltpu.VMEM(keys.shape, BF16),
            pltpu.VMEM(values.shape, BF16),
            pltpu.VMEM(w_query.shape, BF16),
            pltpu.SemaphoreType.DMA((3,)),
            pltpu.VMEM(table.shape, jnp.int32),
            pltpu.VMEM((pdev * smax // GS, GS, flat), F32),
            pltpu.VMEM((pdev * pairs, 2 * residues, 2 * HEAD), BF16),
            pltpu.VMEM((pdev * pairs, 2 * HEAD, 2 * residues), BF16),
            pltpu.VMEM((width, 128), BF16),
            pltpu.VMEM((width, 128), F32),
            pltpu.VMEM((channels, groups * rows), F32),
            pltpu.VMEM((width, groups * rows), BF16),
            pltpu.VMEM((local, groups * rows), BF16),
            pltpu.VMEM((local, groups * rows), BF16),
            pltpu.VMEM((steps, tensors, channels, groups * rows), F32),
            pltpu.VMEM((nodes, 1, flat), F32),
            pltpu.VMEM((nodes, 1, flat), F32),
            pltpu.SemaphoreType.DMA((steps, 2, max(tensors - 1, 1))),
            pltpu.SemaphoreType.DMA((steps, 2, max(tensors - 1, 1))),
            pltpu.SemaphoreType.DMA((nodes - 1,)),
            pltpu.SemaphoreType.DMA((nodes - 1,)),
        ],
        compiler_params=pltpu.CompilerParams(
            collective_id=0, has_side_effects=True, vmem_limit_bytes=60 * 1024 * 1024
        ),
        name="denoise",
    )(
        counts, counts.reshape(1, -1), table.T, z_home, keys, values, w_embed, step_bias,
        ln_gain, w_query, w_out.T,
    )


def solution(mesh):
    return jax.shard_map(
        per_device,
        mesh=mesh,
        in_specs=(
            P("pocket", None, None),
            P(),
            P(),
            P("pocket", "tensor", None),
            P("pocket", "tensor", None),
            P(),
            P(),
            P(),
            P("tensor", None),
            P("tensor", None),
        ),
        out_specs=P("pocket", None),
        check_vma=False,
    )
```

```python
import functools

import jax
import jax.numpy as jnp
from jax import lax
from jax.experimental import pallas as pl
from jax.experimental.pallas import tpu as pltpu
from jax.sharding import PartitionSpec as P

HEAD = 64
CAP = 1
WORK = 36
GS = 8
EPS = 1e-05
F32 = jnp.float32
BF16 = jnp.bfloat16
HIGHEST = lax.Precision.HIGHEST
NT = (((1,), (1,)), ((), ()))
TN = (((0,), (0,)), ((), ()))


def iota(shape, axis):
    return lax.broadcasted_iota(jnp.int32, shape, axis)


def split3(value):
    high = value.astype(BF16).astype(F32)
    rest = value - high
    middle = rest.astype(BF16).astype(F32)
    return high, middle, rest - middle


def kernel(
    dims,
    counts_s, counts_v, table_ref, z_home_ref, keys_hbm, values_hbm, w_embed_ref, step_bias_ref,
    gain_ref, w_query_hbm, w_out_ref, out_ref,
    keys_ref, values_ref, w_query_ref, load, table_s, zf, kbd, vbd, wr, gains, z_ref, normed, queries, attended, part, send, recv,
    psend, precv, fsend, frecv,
):
    nodes, tensors, groups, halves, steps, smax, pdev = dims
    me = lax.axis_index("pocket")
    mt = lax.axis_index("tensor")
    width = w_embed_ref.shape[1]
    channels = w_embed_ref.shape[0]
    atoms = z_home_ref.shape[2] // channels
    local = w_query_ref.shape[0]
    pairs = local // (2 * HEAD)
    rows = GS * atoms
    per = smax // GS
    pockets = nodes * pdev

    barrier = pltpu.get_barrier_semaphore()
    for k in range(1, nodes):
        pl.semaphore_signal(barrier, 1, device_id=(lax.rem(me + k, nodes), mt), device_id_type=pl.DeviceIdType.MESH)
    for k in range(1, tensors):
        pl.semaphore_signal(barrier, 1, device_id=(me, lax.rem(mt + k, tensors)), device_id_type=pl.DeviceIdType.MESH)

    loads = [
        pltpu.make_async_copy(source, target, load.at[k])
        for k, (source, target) in enumerate(
            ((keys_hbm, keys_ref), (values_hbm, values_ref), (w_query_hbm, w_query_ref))
        )
    ]
    for copy in loads:
        copy.start()

    tops = []
    total = 0
    for p in range(pdev):
        total = total + (counts_s[me * pdev + p] + (GS - 1)) // GS
        tops.append(total)

    def place(g):
        pocket = jnp.int32(0)
        first = jnp.int32(0)
        for p in range(pdev - 1):
            past = g >= tops[p]
            pocket = jnp.where(past, p + 1, pocket)
            first = jnp.where(past, tops[p], first)
        block = jnp.clip(g - first, 0, per - 1)
        return pocket, pocket * per + block

    w_mid = w_embed_ref[...] - jnp.mean(w_embed_ref[...], axis=1, keepdims=True)
    bias = step_bias_ref[...] - jnp.mean(step_bias_ref[...], axis=1, keepdims=True)
    gain = gain_ref[...].reshape(1, width)
    padding = jnp.zeros((128 - 6 * (channels + steps), width), F32)

    def stack(weights, biases):
        a, b, c = split3(weights)
        ba, bb, bc = split3(biases)
        return jnp.concatenate([a, b, c, a, b, a, ba, bb, bc, ba, bb, ba, padding], axis=0).T.astype(BF16)

    wr[...] = stack(w_mid, bias)
    gains[...] = stack(w_mid * gain, bias * gain)

    residues = keys_ref.shape[2]
    zeros = jnp.zeros((HEAD, residues), BF16)
    left_head = iota((residues, 2 * HEAD), 1) < HEAD
    for p in range(pdev):
        block = z_home_ref[p].astype(F32)
        for j in range(per):
            zf[p * per + j] = block[j * GS:(j + 1) * GS]

    flat = atoms * channels
    own_atom = iota((rows, flat), 1) // channels == lax.rem(iota((rows, flat), 0), atoms)
    fold = (lax.rem(iota((channels, flat), 1), channels) == iota((channels, flat), 0)).astype(F32)
    for g in range(groups):
        pocket, block = place(jnp.int32(g))
        flat_z = zf[block]
        copies = jnp.broadcast_to(flat_z[:, None, :], (GS, atoms, flat)).reshape(rows, flat)
        copies = jnp.where(own_atom, copies, 0.0).astype(BF16)
        z_ref[:, g * rows:(g + 1) * rows] = lax.dot_general(fold.astype(BF16), copies, NT, preferred_element_type=F32)

    table_s[...] = table_ref[...].astype(F32).T.astype(jnp.int32)
    seats = groups * GS
    slots = -(-WORK // 8) * 8
    lanes = iota((1, seats), 1)
    entry = jnp.full((1, seats), -1, jnp.int32)
    for g in range(groups):
        _, block = place(jnp.int32(g))
        inside = (lanes >= g * GS) & (lanes < (g + 1) * GS) & (g < tops[-1])
        entry = jnp.where(inside, block * GS + lanes - g * GS, entry)
    keep_rows = jnp.zeros((slots, seats), F32)
    send_rows = jnp.zeros((nodes, seats), F32)
    for p in range(pdev):
        target = table_s[pl.ds(me * pdev + p, 1), :]
        alive = iota((1, smax), 1) < counts_s[me * pdev + p]
        target = jnp.where(alive, target, -1)
        matches = (iota((smax, seats), 0) + p * smax == entry).astype(F32)
        stay = (iota((slots, smax), 0) == target - me * WORK) & (iota((slots, smax), 0) < WORK)
        keep_rows = keep_rows + jnp.dot(stay.astype(F32), matches, preferred_element_type=F32)
        node = iota((nodes, smax), 0)
        leave = (target >= node * WORK) & (target < node * WORK + WORK) & (node != me)
        send_rows = send_rows + jnp.dot(leave.astype(F32), matches, preferred_element_type=F32)
    diagonal = iota((pockets, pockets), 0) == iota((pockets, pockets), 1)
    count_rows = jnp.sum(jnp.where(diagonal, counts_v[...].astype(F32), 0.0), axis=1, keepdims=True)
    here = table_s[...] - me * WORK
    whose = iota((pockets, smax), 0)
    arrives = (
        (iota((pockets, smax), 1).astype(F32) < count_rows)
        & (here >= 0) & (here < WORK)
        & ((whose < me * pdev) | (whose >= me * pdev + pdev))
    )
    arrival = jnp.max(jnp.where(arrives, here.astype(F32), -1.0), axis=1, keepdims=True)
    by_pocket = (arrival == iota((pockets, slots), 1).astype(F32)).astype(F32)
    pocket_id = iota((pockets, nodes), 0)
    node_id = iota((pockets, nodes), 1) * pdev
    by_node = ((pocket_id >= node_id) & (pocket_id < node_id + pdev)).astype(F32)
    take_rows = lax.dot_general(by_pocket, by_node, TN, preferred_element_type=F32)

    loads[0].wait()
    loads[1].wait()
    for p in range(pdev):
        for hp in range(pairs):
            i = p * pairs + hp
            turned = (keys_ref[p, hp * 2 * HEAD:(hp + 1) * 2 * HEAD, :].astype(F32) * 0.125).T
            kbd[i, :residues, :] = jnp.where(left_head, turned, 0.0).astype(BF16)
            kbd[i, residues:, :] = jnp.where(left_head, 0.0, turned).astype(BF16)
            for side in range(2):
                inner = slice(side * HEAD, (side + 1) * HEAD)
                outer = slice(hp * 2 * HEAD + side * HEAD, hp * 2 * HEAD + (side + 1) * HEAD)
                vbd[i, inner, side * residues:(side + 1) * residues] = values_ref[p, outer, :]
                vbd[i, inner, (1 - side) * residues:(2 - side) * residues] = zeros

    loads[2].wait()
    pl.semaphore_wait(barrier, nodes + tensors - 2)


    def exchange(t, h, k):
        first, count = halves[h]
        here = part.at[t, mt, :, first * rows:(first + count) * rows]
        return pltpu.make_async_remote_copy(
            src_ref=here, dst_ref=here, send_sem=psend.at[t, h, k - 1], recv_sem=precv.at[t, h, k - 1],
            device_id=(me, lax.rem(mt + k, tensors)), device_id_type=pl.DeviceIdType.MESH,
        )

    def pick(t, table):
        value = jnp.float32(table[-1])
        for k in range(steps - 1):
            value = jnp.where(t == k, jnp.float32(table[k]), value)
        return value

    keeps = [0.95 + 0.01 * k for k in range(steps)]
    pushes = [-0.8 + 0.1 * k for k in range(steps)]

    def update(t, h):
        first, count = halves[h]
        for k in range(1, tensors):
            exchange(t, h, k).wait()
        window = slice(first * rows, (first + count) * rows)
        guess = part[t, 0, :, window]
        for k in range(1, tensors):
            guess = guess + part[t, k, :, window]
        z_ref[:, window] = pick(t, keeps) * z_ref[:, window] + pick(t, pushes) * guess

    def compute(t, h):
        first, count = halves[h]

        window = slice(first * rows, (first + count) * rows)
        for start in range(first, first + count, 2):
            span = min(2, first + count - start)
            some = slice(start * rows, (start + span) * rows)
            high, middle, low = split3(z_ref[:, some])
            rest_id = iota((128 - 6 * channels, span * rows), 0)
            flags = ((lax.rem(rest_id, steps) == t) & (rest_id < 3 * steps)).astype(F32)
            right = jnp.concatenate([high, high, high, middle, middle, low, flags], axis=0).astype(BF16)
            total_sq = jnp.zeros((1, span * rows), F32)
            chunk = width // 4
            for f in range(0, width, chunk):
                centred = jnp.dot(wr[f:f + chunk, :], right, preferred_element_type=F32)
                total_sq = total_sq + jnp.sum(centred * centred, axis=0, keepdims=True)
            scale = lax.rsqrt(total_sq * (1.0 / width) + EPS)
            high, middle, low = split3(z_ref[:, some] * scale)
            s_high, s_middle, s_low = split3(scale)
            scales = jnp.where(rest_id < 3 * steps, s_high, jnp.where(rest_id < 5 * steps, s_middle, s_low))
            mine = (lax.rem(rest_id, steps) == t) & (rest_id < 6 * steps)
            right = jnp.concatenate(
                [high, high, high, middle, middle, low, jnp.where(mine, scales, 0.0)], axis=0
            ).astype(BF16)
            for f in range(0, width, chunk):
                normed[f:f + chunk, some] = jnp.dot(
                    gains[f:f + chunk, :], right, preferred_element_type=F32
                ).astype(BF16)
        queries[:, window] = jnp.dot(w_query_ref[...], normed[:, window], preferred_element_type=F32).astype(BF16)

        for g in range(first, first + count):
            lanes_g = slice(g * rows, (g + 1) * rows)
            pocket, _ = place(jnp.int32(g))
            for hp in range(pairs):
                cols = slice(hp * 2 * HEAD, (hp + 1) * 2 * HEAD)
                scores = jnp.dot(kbd[pocket * pairs + hp], queries[cols, lanes_g], preferred_element_type=F32)
                s0 = scores[:residues]
                s1 = scores[residues:]
                e0 = jnp.exp(s0 - jnp.max(s0, axis=0, keepdims=True))
                e1 = jnp.exp(s1 - jnp.max(s1, axis=0, keepdims=True))
                r0 = 1.0 / jnp.sum(e0, axis=0, keepdims=True)
                r1 = 1.0 / jnp.sum(e1, axis=0, keepdims=True)
                e = jnp.concatenate([e0.astype(BF16), e1.astype(BF16)], axis=0)
                mixed = jnp.dot(vbd[pocket * pairs + hp], e, preferred_element_type=F32)
                attended[hp * 2 * HEAD:hp * 2 * HEAD + HEAD, lanes_g] = (mixed[:HEAD] * r0).astype(BF16)
                attended[hp * 2 * HEAD + HEAD:(hp + 1) * 2 * HEAD, lanes_g] = (mixed[HEAD:] * r1).astype(BF16)
        part[t, mt, :, window] = jnp.dot(w_out_ref[...], attended[:, window], preferred_element_type=F32)
        for k in range(1, tensors):
            exchange(t, h, k).start()

    for h in range(len(halves)):
        compute(0, h)

    def step(t, carry):
        for h in range(len(halves)):
            update(t - 1, h)
            compute(t, h)
        return carry

    lax.fori_loop(1, steps, step, 0)

    for h in range(len(halves)):
        update(steps - 1, h)
    done = []
    for g in range(groups):
        wide = lax.dot_general(
            z_ref[:, g * rows:(g + 1) * rows], fold, TN, precision=HIGHEST, preferred_element_type=F32
        )
        done.append(jnp.sum(jnp.where(own_atom, wide, 0.0).reshape(GS, atoms, flat), axis=1))
    done = jnp.concatenate(done, axis=0)
    leaving = jnp.dot(send_rows, done, precision=HIGHEST, preferred_element_type=F32)
    for d in range(nodes):
        send[d] = leaving[d:d + 1]

    def hand(k):
        peer = lax.rem(me + k, nodes)
        return pltpu.make_async_remote_copy(
            src_ref=send.at[peer], dst_ref=recv.at[me], send_sem=fsend.at[k - 1], recv_sem=frecv.at[k - 1],
            device_id=(peer, mt), device_id_type=pl.DeviceIdType.MESH,
        )

    for k in range(1, nodes):
        hand(k).start()
    recv[me] = jnp.zeros((1, flat), F32)
    result = jnp.dot(keep_rows, done, precision=HIGHEST, preferred_element_type=F32)
    for k in range(1, nodes):
        hand(k).wait()
    landed = recv[...].reshape(nodes, flat)
    result = result + jnp.dot(take_rows, landed, precision=HIGHEST, preferred_element_type=F32)
    out_ref[...] = result[:WORK]


def per_device(z_home, counts, table, keys, values, w_embed, step_bias, ln_gain, w_query, w_out):
    nodes = lax.axis_size("pocket")
    tensors = lax.axis_size("tensor")
    pdev, smax, flat = z_home.shape
    channels, width = w_embed.shape
    atoms = flat // channels
    steps = step_bias.shape[0]
    local = w_query.shape[0]
    pairs = local // (2 * HEAD)
    residues = keys.shape[2]
    heavy = WORK + CAP * nodes // 2
    light = WORK - CAP * nodes // 2
    groups = max(
        smax // GS + (heavy - smax + (pdev - 1) * (GS - 1)) // GS,
        (light + pdev * (GS - 1)) // GS,
    )
    rows = GS * atoms
    front = (groups + 1) // 2
    halves = ((0, front), (front, groups - front))
    dims = (nodes, tensors, groups, halves, steps, smax, pdev)
    vmem = pl.BlockSpec(memory_space=pltpu.VMEM)
    smem = pl.BlockSpec(memory_space=pltpu.SMEM)
    hbm = pl.BlockSpec(memory_space=pl.ANY)
    return pl.pallas_call(
        functools.partial(kernel, dims),
        out_shape=jax.ShapeDtypeStruct((WORK, flat), F32),
        in_specs=[smem] + [vmem] * 3 + [hbm] * 2 + [vmem] * 3 + [hbm, vmem],
        out_specs=vmem,
        scratch_shapes=[
            pltpu.VMEM(keys.shape, BF16),
            pltpu.VMEM(values.shape, BF16),
            pltpu.VMEM(w_query.shape, BF16),
            pltpu.SemaphoreType.DMA((3,)),
            pltpu.VMEM(table.shape, jnp.int32),
            pltpu.VMEM((pdev * smax // GS, GS, flat), F32),
            pltpu.VMEM((pdev * pairs, 2 * residues, 2 * HEAD), BF16),
            pltpu.VMEM((pdev * pairs, 2 * HEAD, 2 * residues), BF16),
            pltpu.VMEM((width, 128), BF16),
            pltpu.VMEM((width, 128), BF16),
            pltpu.VMEM((channels, groups * rows), F32),
            pltpu.VMEM((width, groups * rows), BF16),
            pltpu.VMEM((local, groups * rows), BF16),
            pltpu.VMEM((local, groups * rows), BF16),
            pltpu.VMEM((steps, tensors, channels, groups * rows), F32),
            pltpu.VMEM((nodes, 1, flat), F32),
            pltpu.VMEM((nodes, 1, flat), F32),
            pltpu.SemaphoreType.DMA((steps, 2, max(tensors - 1, 1))),
            pltpu.SemaphoreType.DMA((steps, 2, max(tensors - 1, 1))),
            pltpu.SemaphoreType.DMA((nodes - 1,)),
            pltpu.SemaphoreType.DMA((nodes - 1,)),
        ],
        compiler_params=pltpu.CompilerParams(
            collective_id=0, has_side_effects=True, vmem_limit_bytes=60 * 1024 * 1024
        ),
        name="denoise",
    )(
        counts, counts.reshape(1, -1), table.T, z_home, keys, values, w_embed, step_bias,
        ln_gain, w_query, w_out.T,
    )


def solution(mesh):
    return jax.shard_map(
        per_device,
        mesh=mesh,
        in_specs=(
            P("pocket", None, None),
            P(),
            P(),
            P("pocket", "tensor", None),
            P("pocket", "tensor", None),
            P(),
            P(),
            P(),
            P("tensor", None),
            P("tensor", None),
        ),
        out_specs=P("pocket", None),
        check_vma=False,
    )
```
